32 devices in a mesh: gx: 4 (over z), gy: 8 (over y, x, core).
Axes of the slice: x: 2, y: 2, z: 4, core: 2. Of those that a mesh axis runs over, the one named last changes fastest.
Arguments:
- tokens: bfloat16 [512, 3584], P(('gx', 'gy')), may hold values from -6 to 6
- expert_ids: int32 [512, 8], P(('gx', 'gy')), may hold values from 0 to 31, all different within a row; in each aligned block of 16 rows (0 to 15, 16 to 31, ...) at most 6 rows name the same one
- backup_ids: int32 [512, 8], P(('gx', 'gy')), may hold values from 0 to 31, all different within a row; in each aligned block of 16 rows (0 to 15, 16 to 31, ...) at most 6 rows name the same one
- scores: float32 [512, 8], P(('gx', 'gy')), may hold values from 0.05 to 1
- gate_weight: bfloat16 [32, 3584, 1024], P(('gx', 'gy')), may hold values from -0.09375 to 0.09375
- up_weight: bfloat16 [32, 3584, 1024], P(('gx', 'gy')), may hold values from -0.09375 to 0.09375
- down_weight: bfloat16 [32, 1024, 3584], P(('gx', 'gy')), may hold values from -0.1875 to 0.1875
Outputs:
- mixed: bfloat16 [512, 3584], P(('gx', 'gy'))
The draws below stay inside these ranges and needn't reach their ends.
Inputs may be any that keep to these rules, and one draw needn't show every extreme that they name: `expert_ids`: among the rows of one device no expert number is named more than 6 times. `backup_ids`: among the rows of one device no expert number is named more than 6 times.
All inputs are finite; a program needn't handle non-finite values.
Results may differ from the reference program's by a relative error of at most 0.0058.
Values may be sent and summed in bfloat16 or wider, within the bound.
A program may use at most 128 MiB of HBM per device.

```python
import math
import jax
import jax.numpy as jnp
import numpy as np
from jax import lax

D = 3584
FF = 1024
TOP = 8
TOK_DEV = 16
EXPERTS = 32
TOKENS = 512
MOST = 6
CAP = 128
QUOTA = 1
SPARE = 32


def level_of(stream_key, shape, cuts, low, top_value):
    factor_of, own = 1.0, jax.random.fold_in(stream_key, 6)
    for axis_at, parts in cuts:
        heights = jnp.exp(jax.random.uniform(jax.random.fold_in(own, axis_at), (parts,), jnp.float32, low / len(cuts), top_value / len(cuts)))
        factor_of = factor_of * jnp.repeat(heights, shape[axis_at] // parts).reshape([-1 if axis == axis_at else 1 for axis in range(len(shape))])
    return factor_of


def deal_out(own_key, own, number, rows, count, top, most, lean):
    ranking = jax.random.permutation(own_key, count)
    crowded, common = load_shares(count, rows * top, most, lean, True), load_shares(count, rows * top, most, lean, False)
    places = jnp.arange(count)

    def named(tallies, turn):
        used = int((tallies > 0).sum())
        fixed = max(1, used // 4)
        moved = fixed + (places - fixed + turn * (used - fixed)) % max(1, count - fixed)
        return jnp.zeros((count,), jnp.int32).at[ranking[jnp.where(places < fixed, places, moved)]].set(jnp.asarray(tallies, jnp.int32))

    tallies = jnp.where(number % 4 == 0, named(crowded, number // 4), named(common, number - number // 4 - 1))
    mixed = jax.random.permutation(jax.random.fold_in(own, 3), count)
    donor, taker = mixed[0:count // 2 * 2:2], mixed[1:count // 2 * 2:2]
    room = jnp.minimum(tallies[donor] - 1, most - tallies[taker]) // 2
    room = jnp.where((donor == ranking[0]) | (taker == ranking[0]) | (tallies[taker] == 0), 0, jnp.maximum(room, 0))
    moved = jax.random.randint(jax.random.fold_in(own, 4), (count // 2,), 0, 1 << 20) % (room + 1)
    tallies = tallies.at[donor].add(-moved).at[taker].add(moved)
    labels = jnp.searchsorted(jnp.cumsum(tallies), jnp.arange(rows * top), side="right").astype(jnp.int32)
    table = labels.reshape(top, rows).T
    table = table[jax.random.permutation(jax.random.fold_in(own, 1), rows)]
    turn = jax.random.randint(jax.random.fold_in(own, 2), (rows, 1), 0, top)
    return jnp.take_along_axis(table, (jnp.arange(top)[None, :] + turn) % top, axis=1)


def load_shares(count, total, reach, skew, full):
    weights = [(1 << 20) // math.isqrt(rank ** skew) + 1 for rank in range(1, count + 1)]
    largest = reach if full else min(reach, max(-(-total // count), total * weights[0] // sum(weights)))
    least = 1 if total - largest >= count - 1 else 0
    counts, surplus = [largest] + [least] * (count - 1), total - largest - least * (count - 1)
    while surplus > 0:
        candidates = [i for i in range(1, count) if counts[i] < largest] or [i for i in range(1, count) if counts[i] < reach]
        whole, left = sum([weights[i] for i in candidates]), surplus
        for i in candidates:
            more = min(reach - counts[i], max(1, left * weights[i] // whole), surplus)
            counts[i] = counts[i] + more
            surplus = surplus - more
    return np.array(counts)


def bell_draw(key, dims, deviation, most, shards=(), held_as=jnp.bfloat16):
    result = jax.random.normal(key, dims, jnp.float32) * deviation
    if len(shards) > 0:
        result = level_of(key, dims, shards, -0.22, 0.18) * result
    return jnp.clip(result, min=-most, max=most).astype(held_as)


def setup_inputs(seed: int = 0) -> dict:
    key_list = jax.random.split(jax.random.key(seed), 8)
    tokens = bell_draw(key_list[0], (TOKENS, D), 1.0, 6.0, ((0, 32),))
    expert_ids_keys = jax.random.split(jax.random.fold_in(key_list[1], 1), TOKENS // TOK_DEV)
    expert_ids_turns = jax.random.permutation(jax.random.fold_in(key_list[1], 3), TOKENS // TOK_DEV)
    expert_ids = jax.vmap(lambda own, number: deal_out(jax.random.fold_in(key_list[1], 2), own, number, TOK_DEV, EXPERTS, TOP, MOST, 2))(expert_ids_keys, expert_ids_turns).reshape((TOKENS, TOP))
    backup_ids_keys = jax.random.split(jax.random.fold_in(key_list[2], 1), TOKENS // TOK_DEV)
    backup_ids_turns = jax.random.permutation(jax.random.fold_in(key_list[2], 3), TOKENS // TOK_DEV)
    backup_ids = jax.vmap(lambda own, number: deal_out(jax.random.fold_in(key_list[2], 2), own, number, TOK_DEV, EXPERTS, TOP, MOST, 0))(backup_ids_keys, backup_ids_turns).reshape((TOKENS, TOP))
    scores = jnp.clip(jnp.exp(math.log(1.0) - 2.9957323 * jax.random.uniform(key_list[3], (TOKENS, TOP), jnp.float32) ** level_of(key_list[3], (TOKENS, TOP), ((0, 32),), -0.2, 0.2)), 0.05, 1.0)
    gate_weight = bell_draw(key_list[4], (EXPERTS, D, FF), D ** -0.5, 0.09375, ((0, 32),))
    up_weight = bell_draw(key_list[5], (EXPERTS, D, FF), D ** -0.5, 0.09375, ((0, 32),))
    down_weight = bell_draw(key_list[6], (EXPERTS, FF, D), FF ** -0.5, 0.1875, ((0, 32),))
    return dict(tokens=tokens, expert_ids=expert_ids, backup_ids=backup_ids, scores=scores, gate_weight=gate_weight, up_weight=up_weight, down_weight=down_weight)


def ranks_in_order(numbers, active):
    table = ((numbers[:, None] == jnp.arange(EXPERTS, dtype=jnp.int32)[None, :]) & active[:, None]).astype(jnp.int32)
    before = jnp.cumsum(table, axis=0) - table
    return jnp.sum(before * table, axis=1).astype(jnp.int32)


def reference(tokens, expert_ids, backup_ids, scores, gate_weight, up_weight, down_weight):
    choices = TOKENS * TOP
    per_source = TOK_DEV * TOP
    slots = CAP + SPARE
    first_flat = expert_ids.reshape(-1).astype(jnp.int32)
    backup_flat = backup_ids.reshape(-1).astype(jnp.int32)
    first_rank = ranks_in_order(first_flat, jnp.ones((choices,), dtype=bool))
    kept = first_rank < CAP
    spilled = jnp.logical_not(kept)
    spill_rank = jax.vmap(ranks_in_order)(backup_flat.reshape(EXPERTS, per_source),
                                          spilled.reshape(EXPERTS, per_source)).reshape(-1).astype(jnp.int32)
    spare_ok = spilled & (spill_rank < QUOTA)
    source_device = (jnp.arange(choices, dtype=jnp.int32) // per_source).astype(jnp.int32)
    outside = EXPERTS * slots
    target = jnp.where(kept, first_flat * slots + first_rank,
                       jnp.where(spare_ok, backup_flat * slots + CAP + source_device * QUOTA + spill_rank,
                                 outside)).astype(jnp.int32)
    sources = jnp.full((outside,), -1, dtype=jnp.int32)
    sources = sources.at[target].set(jnp.arange(choices, dtype=jnp.int32), mode="drop").reshape(EXPERTS, slots)

    def expert_block(inputs):
        source_list, w_gate, w_up, w_down = inputs
        token_index = (jnp.maximum(source_list, 0) // TOP).astype(jnp.int32)
        rows = jnp.where((source_list >= 0)[:, None], tokens[token_index], jnp.zeros((), jnp.bfloat16))
        gate = jnp.dot(rows, w_gate, preferred_element_type=jnp.float32)
        upward = jnp.dot(rows, w_up, preferred_element_type=jnp.float32)
        hidden = (jax.nn.silu(gate) * upward).astype(jnp.bfloat16)
        return jnp.dot(hidden, w_down, preferred_element_type=jnp.float32).astype(jnp.bfloat16)

    outputs = lax.map(expert_block, (sources, gate_weight, up_weight, down_weight))
    flat_out = outputs.reshape(outside, D)
    picked = jnp.take(flat_out, jnp.minimum(target, outside - 1), axis=0)
    valid = (kept | spare_ok).reshape(TOKENS, TOP)
    route_weights = scores / jnp.sum(scores, axis=1, keepdims=True)
    weights = jnp.where(valid, route_weights, jnp.zeros((), jnp.float32))
    mixed = jnp.sum(weights[:, :, None] * picked.reshape(TOKENS, TOP, D).astype(jnp.float32), axis=1)
    return mixed.astype(jnp.bfloat16)
```

```python
import functools
import jax
import jax.numpy as jnp
from jax import lax
from jax.experimental import pallas as pl
from jax.experimental.pallas import tpu as pltpu
from jax.sharding import PartitionSpec as P


def ranks_within(numbers, active, expert_count):
    table = (
        (numbers[:, None] == jnp.arange(expert_count, dtype=jnp.int32)[None, :]) & active[:, None]
    ).astype(jnp.int32)
    within = jnp.sum((jnp.cumsum(table, axis=0) - table) * table, axis=1)
    return (within, table)


def pack_rows(tokens, destination, active, slot_total, top_count):
    pick_number = jnp.arange(destination.shape[0], dtype=jnp.int32)
    match_grid = (
        destination[None, :] == jnp.arange(slot_total, dtype=jnp.int32)[:, None]
    ) & active[None, :]
    source = jnp.sum(jnp.where(match_grid, pick_number[None, :] + 1, 0), axis=1) - 1
    picked_rows = jnp.take(tokens, jnp.maximum(source, 0) // top_count, axis=0)
    return jnp.where((source >= 0)[:, None], picked_rows, jnp.zeros((), tokens.dtype))


def send_rows(slot_rows):
    return lax.all_to_all(slot_rows, ("gx", "gy"), split_axis=0, concat_axis=0, tiled=True)


def on_device(tokens, expert_ids, backup_ids, scores, gate_weight, up_weight, down_weight):
    device_count = lax.axis_size(("gx", "gy"))
    own_index = lax.axis_index(("gx", "gy"))
    tok_rows, top_count = expert_ids.shape
    model_width = tokens.shape[1]
    per_source = tok_rows * top_count
    spare_quota = max(1, per_source // (4 * device_count))
    most_rows = max(2, (3 * per_source + 2 * device_count - 1) // (2 * device_count))
    first_flat = expert_ids.reshape(-1)
    backup_flat = backup_ids.reshape(-1)
    everyone = jnp.ones((per_source,), dtype=bool)
    first_within, first_table = ranks_within(first_flat, everyone, device_count)
    own_counts = jnp.sum(first_table, axis=0)
    all_counts = lax.all_gather(own_counts[None, :], ("gx", "gy"), axis=0, tiled=True)
    before = jnp.cumsum(all_counts, axis=0) - all_counts
    own_before = lax.dynamic_index_in_dim(before, own_index, 0, keepdims=False)
    first_rank = jnp.sum(first_table * own_before[None, :], axis=1) + first_within
    kept_mask = first_rank < per_source
    spilled = jnp.logical_not(kept_mask)
    spill_rank = ranks_within(backup_flat, spilled, device_count)[0]
    spare_mask = spilled & (spill_rank < spare_quota)
    send_first = pack_rows(
        tokens,
        first_flat * most_rows + first_within,
        kept_mask,
        device_count * most_rows,
        top_count,
    ).reshape(device_count, most_rows, model_width)
    send_spill = pack_rows(
        tokens,
        backup_flat * spare_quota + spill_rank,
        spare_mask,
        device_count * spare_quota,
        top_count,
    ).reshape(device_count, spare_quota, model_width)
    recv_first = send_rows(send_first)
    recv_spill = send_rows(send_spill)
    count_column = lax.dynamic_index_in_dim(all_counts, own_index, 1, keepdims=False)
    before_column = lax.dynamic_index_in_dim(before, own_index, 1, keepdims=False)
    ending = before_column + count_column
    row_number = jnp.arange(per_source, dtype=jnp.int32)
    source_of_row = jnp.sum((ending[None, :] <= row_number[:, None]).astype(jnp.int32), axis=1)
    owner_grid = source_of_row[:, None] == jnp.arange(device_count, dtype=jnp.int32)[None, :]
    start_of_row = jnp.sum(jnp.where(owner_grid, before_column[None, :], 0), axis=1)
    filled = row_number < ending[device_count - 1]
    slot_index = jnp.minimum(source_of_row, device_count - 1) * most_rows + jnp.clip(
        row_number - start_of_row, 0, most_rows - 1
    )
    first_rows = jnp.take(
        recv_first.reshape(device_count * most_rows, model_width), slot_index, axis=0
    )
    first_rows = jnp.where(filled[:, None], first_rows, jnp.zeros((), first_rows.dtype))
    expert_rows = jnp.concatenate(
        [first_rows, recv_spill.reshape(device_count * spare_quota, model_width)], axis=0
    )
    gate = jnp.dot(expert_rows, gate_weight[0], preferred_element_type=jnp.float32)
    upward = jnp.dot(expert_rows, up_weight[0], preferred_element_type=jnp.float32)
    hidden = (jax.nn.silu(gate) * upward).astype(jnp.bfloat16)
    expert_out = jnp.dot(hidden, down_weight[0], preferred_element_type=jnp.float32).astype(
        jnp.bfloat16
    )
    position = jnp.arange(most_rows, dtype=jnp.int32)
    rank_grid = before_column[:, None] + position[None, :]
    live_slot = (position[None, :] < count_column[:, None]) & (rank_grid < per_source)
    back_first = jnp.take(expert_out[:per_source], jnp.clip(rank_grid, 0, per_source - 1), axis=0)
    back_first = jnp.where(live_slot[:, :, None], back_first, jnp.zeros((), back_first.dtype))
    back_spill = expert_out[per_source:].reshape(device_count, spare_quota, model_width)
    home_first = send_rows(back_first)
    home_spill = send_rows(back_spill)
    first_slot = jnp.minimum(first_flat * most_rows + first_within, device_count * most_rows - 1)
    spill_slot = backup_flat * spare_quota + jnp.minimum(spill_rank, spare_quota - 1)
    picked_first = jnp.take(
        home_first.reshape(device_count * most_rows, model_width), first_slot, axis=0
    )
    picked_spill = jnp.take(
        home_spill.reshape(device_count * spare_quota, model_width), spill_slot, axis=0
    )
    picked = jnp.where(kept_mask[:, None], picked_first, picked_spill).reshape(
        tok_rows, top_count, model_width
    )
    route_weights = scores / jnp.sum(scores, axis=1, keepdims=True)
    weights = jnp.where(
        (kept_mask | spare_mask).reshape(tok_rows, top_count),
        route_weights,
        jnp.zeros((), jnp.float32),
    )
    mixed = jnp.sum(weights[:, :, None] * picked.astype(jnp.float32), axis=1)
    return mixed.astype(jnp.bfloat16)


def exchange(cfg, tok_ref, meta_ref, gate_hbm, up_hbm, down_hbm, out_ref,
             metas, toks, wg, wu, wd, pick, comb_hi, comb_lo, gate, upward, hidden,
             own, to_core, from_core, to_one, from_one, to_two, from_two, to_z, from_z,
             ag_send, ag_recv, rs_send, rs_recv, w_sem):
    parts, width, cap, quota, slots, top = cfg
    z = lax.axis_index("gx")
    g = lax.axis_index("gy")
    c = lax.rem(g, 2)
    x = lax.rem(lax.div(g, 2), 2)
    y = lax.div(g, 4)
    core_peer = (z, g + 1 - 2 * c)
    x_peer = (z, g + 2 - 4 * x)
    y_peer = (z, g + 4 - 8 * y)
    z_peers = [(lax.rem(z + hop, 4), g) for hop in (1, 2, 3)]
    expert = z * 8 + g

    def remote(src, dst, sems, device):
        return pltpu.make_async_remote_copy(
            src_ref=src, dst_ref=dst, send_sem=sems[0], recv_sem=sems[1],
            device_id=device, device_id_type=pl.DeviceIdType.MESH)

    weight_copies = []
    for j in range(parts):
        rows = pl.ds(j * width, width)
        pair = [pltpu.make_async_copy(gate_hbm.at[0, rows], wg.at[rows], w_sem.at[0, j]),
                pltpu.make_async_copy(up_hbm.at[0, rows], wu.at[rows], w_sem.at[1, j])]
        weight_copies.append(pair)
        for copy in pair:
            copy.start()
    down_copies = []
    for j in range(parts):
        copy = pltpu.make_async_copy(down_hbm.at[0, :, pl.ds(j * width, width)], wd.at[j], w_sem.at[2, j])
        copy.start()
        down_copies.append(copy)

    barrier = pltpu.get_barrier_semaphore()
    for peer in [core_peer, x_peer, y_peer] + z_peers:
        pl.semaphore_signal(barrier, inc=1, device_id=peer, device_id_type=pl.DeviceIdType.MESH)
    metas[z, y, x, c] = meta_ref[...]
    for j in range(parts):
        toks[j, z, y, x, c] = tok_ref[:, j * width:(j + 1) * width]
    pl.semaphore_wait(barrier, 6)

    items = [metas] + [toks.at[j] for j in range(parts)]
    started = []

    def gather_copies(i):
        buf = items[i]
        sem = lambda k: (ag_send.at[i, k], ag_recv.at[i, k])
        mine = buf.at[z, y, x, c]
        copies = [[remote(mine, mine, sem(k), z_peers[k]) for k in range(3)]]
        line = buf.at[:, y, x, c]
        if i % 2 == 0:
            plane = buf.at[:, y, :, c]
            copies += [[remote(line, line, sem(3), x_peer)], [remote(plane, plane, sem(4), y_peer)]]
        else:
            plane = buf.at[:, :, x, c]
            copies += [[remote(line, line, sem(3), y_peer)], [remote(plane, plane, sem(4), x_peer)]]
        whole = buf.at[:, :, :, c]
        copies += [[remote(whole, whole, sem(5), core_peer)]]
        return copies

    gathers = [gather_copies(i) for i in range(len(items))]

    def begin(group):
        for copy in group:
            copy.start()
            started.append(copy)

    def arrive(group):
        for copy in group:
            copy.wait_recv()

    def route():
        record = metas[...].reshape(512, 128)
        first, backup, weight = record[:, 0:top], record[:, top:2 * top], record[:, 2 * top:3 * top]
        lane = lax.broadcasted_iota(jnp.int32, (512, 128), 1).astype(jnp.float32)
        named = jnp.zeros((512, 128), jnp.float32)
        for k in range(top):
            named += jnp.where(first[:, k:k + 1] == lane, 1.0, 0.0)
        row = lax.broadcasted_iota(jnp.int32, (512, 512), 0)
        col = lax.broadcasted_iota(jnp.int32, (512, 512), 1)
        lower = jnp.where(col < row, 1.0, 0.0)
        rank = jnp.dot(lower.astype(jnp.bfloat16), named.astype(jnp.bfloat16), preferred_element_type=jnp.float32)
        spilled = jnp.where(rank >= cap, named, 0.0)
        me = expert.astype(jnp.float32)
        is_me = jnp.where(lane == me, 1.0, 0.0)
        my_named = jnp.sum(is_me * named, axis=1, keepdims=True)
        my_rank = jnp.sum(is_me * rank, axis=1, keepdims=True)
        my_weight = jnp.sum(jnp.where(first == me, weight, 0.0), axis=1, keepdims=True)
        has_backup = jnp.sum(jnp.where(backup == me, 1.0, 0.0), axis=1, keepdims=True)
        its_first = jnp.sum(jnp.where(backup == me, first, 0.0), axis=1, keepdims=True)
        its_weight = jnp.sum(jnp.where(backup == me, weight, 0.0), axis=1, keepdims=True)
        moved = has_backup * jnp.sum(jnp.where(lane == its_first, spilled, 0.0), axis=1, keepdims=True)
        near = jnp.where(lax.div(row, 16) == lax.div(col, 16), lower, 0.0)
        moved_wide = jnp.broadcast_to(moved, (512, 128))
        spill_rank = jnp.dot(near.astype(jnp.bfloat16), moved_wide.astype(jnp.bfloat16),
                             preferred_element_type=jnp.float32)
        block = lax.div(lax.broadcasted_iota(jnp.int32, (512, 128), 0), 16).astype(jnp.float32)
        kept_grid = jnp.where(my_rank == lane, my_named, 0.0)
        spare_grid = jnp.where(spill_rank < quota, jnp.where(block * quota + spill_rank == lane, moved_wide, 0.0), 0.0)
        grid = jnp.concatenate([kept_grid, spare_grid], axis=1)
        pick[...] = grid.T[:slots].astype(jnp.bfloat16)
        mixing = jnp.concatenate([kept_grid * my_weight, spare_grid * its_weight], axis=1)[:, :slots]
        high = mixing.astype(jnp.bfloat16)
        comb_hi[...] = high.reshape(16, 2, 16, slots)
        comb_lo[...] = (mixing - high.astype(jnp.float32)).astype(jnp.bfloat16).reshape(16, 2, 16, slots)

    def project(j):
        for copy in weight_copies[j]:
            copy.wait()
        rows = jnp.dot(pick[...], toks[j].reshape(512, width), preferred_element_type=jnp.float32).astype(jnp.bfloat16)
        part = pl.ds(j * width, width)
        new_gate = jnp.dot(rows, wg[part, :], preferred_element_type=jnp.float32)
        new_up = jnp.dot(rows, wu[part, :], preferred_element_type=jnp.float32)
        if j == 0:
            gate[...] = new_gate
            upward[...] = new_up
        elif j < parts - 1:
            gate[...] += new_gate
            upward[...] += new_up
        else:
            full = gate[...] + new_gate
            hidden[...] = (full / (1.0 + jnp.exp(-full)) * (upward[...] + new_up)).astype(jnp.bfloat16)

    count = len(items)
    for step in range(count + 4):
        if step < count:
            begin(gathers[step][0])
        for stage in (1, 2, 3):
            i = step - stage
            if 0 <= i < count:
                arrive(gathers[i][stage - 1])
                begin(gathers[i][stage])
        i = step - 4
        if 0 <= i < count:
            arrive(gathers[i][3])
            if i == 0:
                route()
            else:
                project(i - 1)

    def scatter_copies(j):
        sem = lambda k: (rs_send.at[j, k], rs_recv.at[j, k])
        one, two = (y_peer, x_peer) if j % 2 == 0 else (x_peer, y_peer)
        return [[remote(to_core.at[j], from_core.at[j], sem(0), core_peer)],
                [remote(to_one.at[j], from_one.at[j], sem(1), one)],
                [remote(to_two.at[j], from_two.at[j], sem(2), two)],
                [remote(to_z.at[j, k], from_z.at[j, k], sem(3 + k), z_peers[k]) for k in range(3)]]

    scatters = [scatter_copies(j) for j in range(parts)]
    f32 = jnp.float32

    def produce(j):
        down_copies[j].wait()
        rows = jnp.dot(hidden[...], wd[j], preferred_element_type=f32).astype(jnp.bfloat16)

        def combine(core):
            high = comb_hi[:, core].reshape(256, slots)
            low = comb_lo[:, core].reshape(256, slots)
            return (jnp.dot(high, rows, preferred_element_type=f32) + jnp.dot(low, rows, preferred_element_type=f32))

        to_core[j] = combine(1 - c).astype(jnp.bfloat16).reshape(4, 2, 2, 16, width)
        begin(scatters[j][0])
        own[j] = combine(c).reshape(4, 2, 2, 16, width)

    def at_one(j, zz, first, second):
        yy, xx = (first, second) if j % 2 == 0 else (second, first)
        return own[j, zz, yy, xx] + from_core[j, zz, yy, xx].astype(f32)

    def after_core(j):
        first = y if j % 2 == 0 else x

        @pl.loop(0, 4)
        def _(zz):
            for second in range(2):
                to_one[j, zz, second] = at_one(j, zz, 1 - first, second).astype(jnp.bfloat16)

        begin(scatters[j][1])

    def at_two(j, zz, first, second):
        return at_one(j, zz, first, second) + from_one[j, zz, second].astype(f32)

    def after_one(j):
        first, second = (y, x) if j % 2 == 0 else (x, y)

        @pl.loop(0, 4)
        def _(zz):
            to_two[j, zz] = at_two(j, zz, first, 1 - second).astype(jnp.bfloat16)

        begin(scatters[j][2])

    def at_z(j, zz):
        first, second = (y, x) if j % 2 == 0 else (x, y)
        return at_two(j, zz, first, second) + from_two[j, zz].astype(f32)

    def after_two(j):
        for k in range(3):
            to_z[j, k] = at_z(j, z_peers[k][0]).astype(jnp.bfloat16)
        begin(scatters[j][3])

    def finish(j):
        total = at_z(j, z)
        for k in range(3):
            total += from_z[j, k].astype(f32)
        out_ref[:, j * width:(j + 1) * width] = total.astype(jnp.bfloat16)

    steps = (after_core, after_one, after_two, finish)
    for step in range(parts + 4):
        if step < parts:
            produce(step)
        for stage in range(4):
            j = step - 1 - stage
            if 0 <= j < parts:
                arrive(scatters[j][stage])
                steps[stage](j)

    for copy in started:
        copy.wait_send()


def fused_body(parts, tokens, expert_ids, backup_ids, scores, gate_weight, up_weight, down_weight):
    device_count = lax.axis_size(("gx", "gy"))
    tok_rows, top = expert_ids.shape
    model, ff = gate_weight.shape[1:]
    cap = tok_rows * top
    quota = max(1, cap // (4 * device_count))
    slots = cap + device_count * quota
    width = model // parts
    route_weights = scores / jnp.sum(scores, axis=1, keepdims=True)
    meta = jnp.concatenate(
        [expert_ids.astype(jnp.float32), backup_ids.astype(jnp.float32), route_weights,
         jnp.zeros((tok_rows, 128 - 3 * top), jnp.float32)], axis=1)
    bf16, f32 = jnp.bfloat16, jnp.float32
    grid = (4, 2, 2)
    vmem = lambda shape, kind: pltpu.VMEM(shape, kind)
    scratch = [
        vmem(grid + (2, tok_rows, 128), f32),
        vmem((parts,) + grid + (2, tok_rows, width), bf16),
        vmem((model, ff), bf16), vmem((model, ff), bf16), vmem((parts, ff, width), bf16),
        vmem((slots, 512), bf16),
        vmem((16, 2, tok_rows, slots), bf16), vmem((16, 2, tok_rows, slots), bf16),
        vmem((slots, ff), f32), vmem((slots, ff), f32), vmem((slots, ff), bf16),
        vmem((parts,) + grid + (tok_rows, width), f32),
        vmem((parts,) + grid + (tok_rows, width), bf16), vmem((parts,) + grid + (tok_rows, width), bf16),
        vmem((parts, 4, 2, tok_rows, width), bf16), vmem((parts, 4, 2, tok_rows, width), bf16),
        vmem((parts, 4, tok_rows, width), bf16), vmem((parts, 4, tok_rows, width), bf16),
        vmem((parts, 3, tok_rows, width), bf16), vmem((parts, 3, tok_rows, width), bf16),
        pltpu.SemaphoreType.DMA((parts + 1, 6)), pltpu.SemaphoreType.DMA((parts + 1, 6)),
        pltpu.SemaphoreType.DMA((parts, 6)), pltpu.SemaphoreType.DMA((parts, 6)),
        pltpu.SemaphoreType.DMA((3, parts)),
    ]
    whole = pl.BlockSpec(memory_space=pltpu.VMEM)
    away = pl.BlockSpec(memory_space=pl.ANY)
    return pl.pallas_call(
        functools.partial(exchange, (parts, width, cap, quota, slots, top)),
        out_shape=jax.ShapeDtypeStruct((tok_rows, model), bf16),
        in_specs=[whole, whole, away, away, away],
        out_specs=whole,
        scratch_shapes=scratch,
        compiler_params=pltpu.CompilerParams(
            collective_id=0, has_side_effects=True, vmem_limit_bytes=60 * 1024 * 1024),
    )(tokens, meta, gate_weight, up_weight, down_weight)


def pick_body(mesh):
    if mesh.shape["gx"] == 4 and mesh.shape["gy"] == 8:
        return functools.partial(fused_body, 4)
    return on_device


def solution(mesh):
    placed = (
        P(("gx", "gy"), None),
        P(("gx", "gy"), None),
        P(("gx", "gy"), None),
        P(("gx", "gy"), None),
        P(("gx", "gy"), None, None),
        P(("gx", "gy"), None, None),
        P(("gx", "gy"), None, None),
    )
    return jax.shard_map(
        pick_body(mesh), mesh=mesh, in_specs=placed, out_specs=P(("gx", "gy"), None), check_vma=False
    )
```

```python
import functools
import jax
import jax.numpy as jnp
from jax import lax
from jax.experimental import pallas as pl
from jax.experimental.pallas import tpu as pltpu
from jax.sharding import PartitionSpec as P


def ranks_within(numbers, active, expert_count):
    table = (
        (numbers[:, None] == jnp.arange(expert_count, dtype=jnp.int32)[None, :]) & active[:, None]
    ).astype(jnp.int32)
    within = jnp.sum((jnp.cumsum(table, axis=0) - table) * table, axis=1)
    return (within, table)


def pack_rows(tokens, destination, active, slot_total, top_count):
    pick_number = jnp.arange(destination.shape[0], dtype=jnp.int32)
    match_grid = (
        destination[None, :] == jnp.arange(slot_total, dtype=jnp.int32)[:, None]
    ) & active[None, :]
    source = jnp.sum(jnp.where(match_grid, pick_number[None, :] + 1, 0), axis=1) - 1
    picked_rows = jnp.take(tokens, jnp.maximum(source, 0) // top_count, axis=0)
    return jnp.where((source >= 0)[:, None], picked_rows, jnp.zeros((), tokens.dtype))


def send_rows(slot_rows):
    return lax.all_to_all(slot_rows, ("gx", "gy"), split_axis=0, concat_axis=0, tiled=True)


def on_device(tokens, expert_ids, backup_ids, scores, gate_weight, up_weight, down_weight):
    device_count = lax.axis_size(("gx", "gy"))
    own_index = lax.axis_index(("gx", "gy"))
    tok_rows, top_count = expert_ids.shape
    model_width = tokens.shape[1]
    per_source = tok_rows * top_count
    spare_quota = max(1, per_source // (4 * device_count))
    most_rows = max(2, (3 * per_source + 2 * device_count - 1) // (2 * device_count))
    first_flat = expert_ids.reshape(-1)
    backup_flat = backup_ids.reshape(-1)
    everyone = jnp.ones((per_source,), dtype=bool)
    first_within, first_table = ranks_within(first_flat, everyone, device_count)
    own_counts = jnp.sum(first_table, axis=0)
    all_counts = lax.all_gather(own_counts[None, :], ("gx", "gy"), axis=0, tiled=True)
    before = jnp.cumsum(all_counts, axis=0) - all_counts
    own_before = lax.dynamic_index_in_dim(before, own_index, 0, keepdims=False)
    first_rank = jnp.sum(first_table * own_before[None, :], axis=1) + first_within
    kept_mask = first_rank < per_source
    spilled = jnp.logical_not(kept_mask)
    spill_rank = ranks_within(backup_flat, spilled, device_count)[0]
    spare_mask = spilled & (spill_rank < spare_quota)
    send_first = pack_rows(
        tokens,
        first_flat * most_rows + first_within,
        kept_mask,
        device_count * most_rows,
        top_count,
    ).reshape(device_count, most_rows, model_width)
    send_spill = pack_rows(
        tokens,
        backup_flat * spare_quota + spill_rank,
        spare_mask,
        device_count * spare_quota,
        top_count,
    ).reshape(device_count, spare_quota, model_width)
    recv_first = send_rows(send_first)
    recv_spill = send_rows(send_spill)
    count_column = lax.dynamic_index_in_dim(all_counts, own_index, 1, keepdims=False)
    before_column = lax.dynamic_index_in_dim(before, own_index, 1, keepdims=False)
    ending = before_column + count_column
    row_number = jnp.arange(per_source, dtype=jnp.int32)
    source_of_row = jnp.sum((ending[None, :] <= row_number[:, None]).astype(jnp.int32), axis=1)
    owner_grid = source_of_row[:, None] == jnp.arange(device_count, dtype=jnp.int32)[None, :]
    start_of_row = jnp.sum(jnp.where(owner_grid, before_column[None, :], 0), axis=1)
    filled = row_number < ending[device_count - 1]
    slot_index = jnp.minimum(source_of_row, device_count - 1) * most_rows + jnp.clip(
        row_number - start_of_row, 0, most_rows - 1
    )
    first_rows = jnp.take(
        recv_first.reshape(device_count * most_rows, model_width), slot_index, axis=0
    )
    first_rows = jnp.where(filled[:, None], first_rows, jnp.zeros((), first_rows.dtype))
    expert_rows = jnp.concatenate(
        [first_rows, recv_spill.reshape(device_count * spare_quota, model_width)], axis=0
    )
    gate = jnp.dot(expert_rows, gate_weight[0], preferred_element_type=jnp.float32)
    upward = jnp.dot(expert_rows, up_weight[0], preferred_element_type=jnp.float32)
    hidden = (jax.nn.silu(gate) * upward).astype(jnp.bfloat16)
    expert_out = jnp.dot(hidden, down_weight[0], preferred_element_type=jnp.float32).astype(
        jnp.bfloat16
    )
    position = jnp.arange(most_rows, dtype=jnp.int32)
    rank_grid = before_column[:, None] + position[None, :]
    live_slot = (position[None, :] < count_column[:, None]) & (rank_grid < per_source)
    back_first = jnp.take(expert_out[:per_source], jnp.clip(rank_grid, 0, per_source - 1), axis=0)
    back_first = jnp.where(live_slot[:, :, None], back_first, jnp.zeros((), back_first.dtype))
    back_spill = expert_out[per_source:].reshape(device_count, spare_quota, model_width)
    home_first = send_rows(back_first)
    home_spill = send_rows(back_spill)
    first_slot = jnp.minimum(first_flat * most_rows + first_within, device_count * most_rows - 1)
    spill_slot = backup_flat * spare_quota + jnp.minimum(spill_rank, spare_quota - 1)
    picked_first = jnp.take(
        home_first.reshape(device_count * most_rows, model_width), first_slot, axis=0
    )
    picked_spill = jnp.take(
        home_spill.reshape(device_count * spare_quota, model_width), spill_slot, axis=0
    )
    picked = jnp.where(kept_mask[:, None], picked_first, picked_spill).reshape(
        tok_rows, top_count, model_width
    )
    route_weights = scores / jnp.sum(scores, axis=1, keepdims=True)
    weights = jnp.where(
        (kept_mask | spare_mask).reshape(tok_rows, top_count),
        route_weights,
        jnp.zeros((), jnp.float32),
    )
    mixed = jnp.sum(weights[:, :, None] * picked.astype(jnp.float32), axis=1)
    return mixed.astype(jnp.bfloat16)


def exchange(cfg, tok_ref, ids_ref, backups_ref, scores_ref, gate_hbm, up_hbm, down_hbm, out_ref,
             flipped, metas, toks, wg, wu, wd, pick, comb_hi, comb_lo, gate, upward, hidden,
             own, to_core, from_core, to_one, from_one, to_two, from_two, to_z, from_z,
             meta_send, meta_recv, ag_send, ag_recv, rs_send, rs_recv, w_sem):
    parts, width, cap, quota, slots, top = cfg
    z = lax.axis_index("gx")
    g = lax.axis_index("gy")
    c = lax.rem(g, 2)
    x = lax.rem(lax.div(g, 2), 2)
    y = lax.div(g, 4)
    core_peer = (z, g + 1 - 2 * c)
    x_peer = (z, g + 2 - 4 * x)
    y_peer = (z, g + 4 - 8 * y)
    z_near = [z + 1 - 2 * lax.rem(z, 2), z + 2 - 4 * lax.div(z, 2), 3 - z]
    z_peers = [(there, g) for there in z_near]
    expert = z * 8 + g

    def remote(src, dst, sems, device):
        return pltpu.make_async_remote_copy(
            src_ref=src, dst_ref=dst, send_sem=sems[0], recv_sem=sems[1],
            device_id=device, device_id_type=pl.DeviceIdType.MESH)

    weight_copies = []
    for j in range(parts):
        rows = pl.ds(j * width, width)
        pair = [pltpu.make_async_copy(gate_hbm.at[0, rows], wg.at[rows], w_sem.at[0, j]),
                pltpu.make_async_copy(up_hbm.at[0, rows], wu.at[rows], w_sem.at[1, j])]
        weight_copies.append(pair)
        for copy in pair:
            copy.start()
    down_copies = []
    for j in range(parts):
        copy = pltpu.make_async_copy(down_hbm.at[0, :, pl.ds(j * width, width)], wd.at[j], w_sem.at[2, j])
        copy.start()
        down_copies.append(copy)

    barrier = pltpu.get_barrier_semaphore()
    for peer in [core_peer, x_peer, y_peer] + z_peers:
        pl.semaphore_signal(barrier, inc=1, device_id=peer, device_id_type=pl.DeviceIdType.MESH)
    scores = scores_ref[...]
    flipped[0:3 * top, 0:16] = jnp.concatenate(
        [ids_ref[...].astype(jnp.float32), backups_ref[...].astype(jnp.float32),
         scores / jnp.sum(scores, axis=0, keepdims=True)], axis=0)
    metas[z, y, x, c] = flipped[...].T[0:16]
    for j in range(parts):
        toks[j, z, y, x, c] = tok_ref[:, j * width:(j + 1) * width]
    pl.semaphore_wait(barrier, 6)

    started = []

    def begin(group):
        for copy in group:
            copy.start()
            started.append(copy)

    def arrive(group):
        for copy in group:
            copy.wait_recv()

    def unit_copies(buf, send, recv, at, zz, flip):
        line, whole = buf.at[zz, y, x, c], buf.at[zz, :, :, c]
        plane = buf.at[zz, :, x, c] if flip else buf.at[zz, y, :, c]
        one, two = (y_peer, x_peer) if flip else (x_peer, y_peer)
        return [[remote(line, line, (send.at[at], recv.at[at]), one)],
                [remote(plane, plane, (send.at[at + 1], recv.at[at + 1]), two)],
                [remote(whole, whole, (send.at[at + 2], recv.at[at + 2]), core_peer)]]

    mine = metas.at[z, y, x, c]
    meta_z = [remote(mine, mine, (meta_send.at[k], meta_recv.at[k]), z_peers[k]) for k in range(3)]
    line, plane, whole = metas.at[:, y, x, c], metas.at[:, y, :, c], metas.at[:, :, :, c]
    meta_rest = [remote(part, part, (meta_send.at[3 + k], meta_recv.at[3 + k]), peer)
                 for k, (part, peer) in enumerate(((line, x_peer), (plane, y_peer), (whole, core_peer)))]
    token_z = []
    for j in range(parts):
        mine = toks.at[j, z, y, x, c]
        token_z.append([remote(mine, mine, (ag_send.at[j, k], ag_recv.at[j, k]), z_peers[k]) for k in range(3)])
    z_order = [z] + z_near
    units = [(p, b) for p in range(parts // 2) for b in range(4)]
    gathers = []
    for p, b in units:
        pair = [unit_copies(toks.at[j], ag_send.at[j], ag_recv.at[j], 3 + 3 * b, z_order[b], j % 2 == 1)
                for j in (2 * p, 2 * p + 1)]
        gathers.append([pair[0][stage] + pair[1][stage] for stage in range(3)])

    def route():
        record = metas[...].reshape(512, 128)
        first, backup, weight = record[:, 0:top], record[:, top:2 * top], record[:, 2 * top:3 * top]
        lane = lax.broadcasted_iota(jnp.int32, (512, 128), 1).astype(jnp.float32)
        named = jnp.zeros((512, 128), jnp.float32)
        for k in range(top):
            named += jnp.where(first[:, k:k + 1] == lane, 1.0, 0.0)
        row = lax.broadcasted_iota(jnp.int32, (512, 512), 0)
        col = lax.broadcasted_iota(jnp.int32, (512, 512), 1)
        lower = jnp.where(col < row, 1.0, 0.0)
        rank = jnp.dot(lower.astype(jnp.bfloat16), named.astype(jnp.bfloat16), preferred_element_type=jnp.float32)
        spilled = jnp.where(rank >= cap, named, 0.0)
        me = expert.astype(jnp.float32)
        is_me = jnp.where(lane == me, 1.0, 0.0)
        my_named = jnp.sum(is_me * named, axis=1, keepdims=True)
        my_rank = jnp.sum(is_me * rank, axis=1, keepdims=True)
        my_weight = jnp.sum(jnp.where(first == me, weight, 0.0), axis=1, keepdims=True)
        has_backup = jnp.sum(jnp.where(backup == me, 1.0, 0.0), axis=1, keepdims=True)
        its_first = jnp.sum(jnp.where(backup == me, first, 0.0), axis=1, keepdims=True)
        its_weight = jnp.sum(jnp.where(backup == me, weight, 0.0), axis=1, keepdims=True)
        moved = has_backup * jnp.sum(jnp.where(lane == its_first, spilled, 0.0), axis=1, keepdims=True)
        near = jnp.where(lax.div(row, 16) == lax.div(col, 16), lower, 0.0)
        moved_wide = jnp.broadcast_to(moved, (512, 128))
        spill_rank = jnp.dot(near.astype(jnp.bfloat16), moved_wide.astype(jnp.bfloat16),
                             preferred_element_type=jnp.float32)
        block = lax.div(lax.broadcasted_iota(jnp.int32, (512, 128), 0), 16).astype(jnp.float32)
        kept_grid = jnp.where(my_rank == lane, my_named, 0.0)
        spare_grid = jnp.where(spill_rank < quota, jnp.where(block * quota + spill_rank == lane, moved_wide, 0.0), 0.0)
        grid = jnp.concatenate([kept_grid, spare_grid], axis=1)
        pick[...] = grid.T[:slots].astype(jnp.bfloat16)
        mixing = jnp.concatenate([kept_grid * my_weight, spare_grid * its_weight], axis=1)[:, :slots]
        high = mixing.astype(jnp.bfloat16)
        comb_hi[...] = high.reshape(16, 2, 16, slots)
        comb_lo[...] = (mixing - high.astype(jnp.float32)).astype(jnp.bfloat16).reshape(16, 2, 16, slots)

    def project(j):
        for copy in weight_copies[j]:
            copy.wait()
        rows = jnp.dot(pick[...], toks[j].reshape(512, width), preferred_element_type=jnp.float32).astype(jnp.bfloat16)
        part = pl.ds(j * width, width)
        new_gate = jnp.dot(rows, wg[part, :], preferred_element_type=jnp.float32)
        new_up = jnp.dot(rows, wu[part, :], preferred_element_type=jnp.float32)
        if j == 0:
            gate[...] = new_gate
            upward[...] = new_up
        elif j < parts - 1:
            gate[...] += new_gate
            upward[...] += new_up
        else:
            full = gate[...] + new_gate
            hidden[...] = (full / (1.0 + jnp.exp(-full)) * (upward[...] + new_up)).astype(jnp.bfloat16)

    begin(meta_z)
    begin(gathers[0][0])
    for p in range(parts // 2):
        for k in range(3):
            begin([token_z[2 * p][k], token_z[2 * p + 1][k]])
    count = len(units)
    for step in range(count + 3):
        if step == 1:
            arrive(meta_z)
            begin(meta_rest[0:1])
        if 2 <= step <= 3:
            arrive(meta_rest[step - 2:step - 1])
            begin(meta_rest[step - 1:step])
        if 0 < step < count:
            p, b = units[step]
            if b > 0:
                arrive([token_z[2 * p][b - 1], token_z[2 * p + 1][b - 1]])
            begin(gathers[step][0])
        for stage in (1, 2):
            i = step - stage
            if 0 <= i < count:
                arrive(gathers[i][stage - 1])
                begin(gathers[i][stage])
        if step == 4:
            arrive(meta_rest[2:3])
            route()
        i = step - 3
        if 0 <= i < count:
            arrive(gathers[i][2])
            if units[i][1] == 3:
                project(2 * units[i][0])
                project(2 * units[i][0] + 1)

    core_copies = [remote(to_core.at[j], from_core.at[j], (rs_send.at[j, 0], rs_recv.at[j, 0]), core_peer)
                   for j in range(parts)]
    back_order = [z_near[2], z_near[1], z_near[0], z]

    def scatter_copies(j, b):
        zz = back_order[b]
        one, two = (y_peer, x_peer) if j % 2 == 0 else (x_peer, y_peer)
        sem = lambda k: (rs_send.at[j, k], rs_recv.at[j, k])
        copies = [remote(to_one.at[j, zz], from_one.at[j, zz], sem(1 + 3 * b), one),
                  remote(to_two.at[j, zz], from_two.at[j, zz], sem(2 + 3 * b), two)]
        if b < 3:
            copies.append(remote(to_z.at[j, b], from_z.at[j, b], sem(3 + 3 * b), z_peers[2 - b]))
        return copies

    scatters = [[scatter_copies(j, b) for j in (2 * p, 2 * p + 1)] for p, b in units]
    f32 = jnp.float32

    def produce(j):
        down_copies[j].wait()
        rows = jnp.dot(hidden[...], wd[j], preferred_element_type=f32).astype(jnp.bfloat16)

        def combine(core):
            high = comb_hi[:, core].reshape(256, slots)
            low = comb_lo[:, core].reshape(256, slots)
            return (jnp.dot(high, rows, preferred_element_type=f32) + jnp.dot(low, rows, preferred_element_type=f32))

        to_core[j] = combine(1 - c).astype(jnp.bfloat16).reshape(4, 2, 2, 16, width)
        begin([core_copies[j]])
        own[j] = combine(c).reshape(4, 2, 2, 16, width)

    def at_one(j, zz, first, second):
        yy, xx = (first, second) if j % 2 == 0 else (second, first)
        return own[j, zz, yy, xx] + from_core[j, zz, yy, xx].astype(f32)

    def after_core(j, zz):
        first = y if j % 2 == 0 else x
        for second in range(2):
            to_one[j, zz, second] = at_one(j, zz, 1 - first, second).astype(jnp.bfloat16)

    def at_two(j, zz, first, second):
        return at_one(j, zz, first, second) + from_one[j, zz, second].astype(f32)

    def after_one(j, zz):
        first, second = (y, x) if j % 2 == 0 else (x, y)
        to_two[j, zz] = at_two(j, zz, first, 1 - second).astype(jnp.bfloat16)

    def at_z(j, zz):
        first, second = (y, x) if j % 2 == 0 else (x, y)
        return at_two(j, zz, first, second) + from_two[j, zz].astype(f32)

    def finish(j):
        total = at_z(j, z)
        for k in range(3):
            total += from_z[j, k].astype(f32)
        out_ref[:, j * width:(j + 1) * width] = total.astype(jnp.bfloat16)

    produce(0)
    produce(1)
    for step in range(count + 3):
        if step < count:
            p, b = units[step]
            if b == 0:
                arrive(core_copies[2 * p:2 * p + 2])
            for h in range(2):
                after_core(2 * p + h, back_order[b])
                begin(scatters[step][h][0:1])
            if b == 1 and 2 * p + 2 < parts:
                produce(2 * p + 2)
                produce(2 * p + 3)
        i = step - 1
        if 0 <= i < count:
            p, b = units[i]
            for h in range(2):
                arrive(scatters[i][h][0:1])
                after_one(2 * p + h, back_order[b])
                begin(scatters[i][h][1:2])
        i = step - 2
        if 0 <= i < count:
            p, b = units[i]
            for h in range(2):
                arrive(scatters[i][h][1:2])
                if b < 3:
                    to_z[2 * p + h, b] = at_z(2 * p + h, back_order[b]).astype(jnp.bfloat16)
                    begin(scatters[i][h][2:3])
        i = step - 3
        if 0 <= i < count and units[i][1] == 3:
            for h in range(2):
                arrive([scatters[i - 3 + k][h][2] for k in range(3)])
                finish(2 * units[i][0] + h)

    for copy in started:
        copy.wait_send()


def fused_body(parts, tokens, expert_ids, backup_ids, scores, gate_weight, up_weight, down_weight):
    device_count = lax.axis_size(("gx", "gy"))
    tok_rows, top = expert_ids.shape
    model, ff = gate_weight.shape[1:]
    cap = tok_rows * top
    quota = max(1, cap // (4 * device_count))
    slots = cap + device_count * quota
    width = model // parts
    bf16, f32 = jnp.bfloat16, jnp.float32
    grid = (4, 2, 2)
    vmem = lambda shape, kind: pltpu.VMEM(shape, kind)
    scratch = [
        vmem((128, 128), f32), vmem(grid + (2, tok_rows, 128), f32),
        vmem((parts,) + grid + (2, tok_rows, width), bf16),
        vmem((model, ff), bf16), vmem((model, ff), bf16), vmem((parts, ff, width), bf16),
        vmem((slots, 512), bf16),
        vmem((16, 2, tok_rows, slots), bf16), vmem((16, 2, tok_rows, slots), bf16),
        vmem((slots, ff), f32), vmem((slots, ff), f32), vmem((slots, ff), bf16),
        vmem((parts,) + grid + (tok_rows, width), f32),
        vmem((parts,) + grid + (tok_rows, width), bf16), vmem((parts,) + grid + (tok_rows, width), bf16),
        vmem((parts, 4, 2, tok_rows, width), bf16), vmem((parts, 4, 2, tok_rows, width), bf16),
        vmem((parts, 4, tok_rows, width), bf16), vmem((parts, 4, tok_rows, width), bf16),
        vmem((parts, 3, tok_rows, width), bf16), vmem((parts, 3, tok_rows, width), bf16),
        pltpu.SemaphoreType.DMA((6,)), pltpu.SemaphoreType.DMA((6,)),
        pltpu.SemaphoreType.DMA((parts, 15)), pltpu.SemaphoreType.DMA((parts, 15)),
        pltpu.SemaphoreType.DMA((parts, 13)), pltpu.SemaphoreType.DMA((parts, 13)),
        pltpu.SemaphoreType.DMA((3, parts)),
    ]
    whole = pl.BlockSpec(memory_space=pltpu.VMEM)
    away = pl.BlockSpec(memory_space=pl.ANY)
    return pl.pallas_call(
        functools.partial(exchange, (parts, width, cap, quota, slots, top)),
        out_shape=jax.ShapeDtypeStruct((tok_rows, model), bf16),
        in_specs=[whole, whole, whole, whole, away, away, away],
        out_specs=whole,
        scratch_shapes=scratch,
        compiler_params=pltpu.CompilerParams(
            collective_id=0, has_side_effects=True, vmem_limit_bytes=60 * 1024 * 1024),
    )(tokens, expert_ids.T, backup_ids.T, scores.T, gate_weight, up_weight, down_weight)


def pick_body(mesh):
    if mesh.shape["gx"] == 4 and mesh.shape["gy"] == 8:
        return functools.partial(fused_body, 2)
    return on_device


def solution(mesh):
    placed = (
        P(("gx", "gy"), None),
        P(("gx", "gy"), None),
        P(("gx", "gy"), None),
        P(("gx", "gy"), None),
        P(("gx", "gy"), None, None),
        P(("gx", "gy"), None, None),
        P(("gx", "gy"), None, None),
    )
    return jax.shard_map(
        pick_body(mesh), mesh=mesh, in_specs=placed, out_specs=P(("gx", "gy"), None), check_vma=False
    )
```

```python
import functools
import jax
import jax.numpy as jnp
from jax import lax
from jax.experimental import pallas as pl
from jax.experimental.pallas import tpu as pltpu
from jax.sharding import PartitionSpec as P


def ranks_within(numbers, active, expert_count):
    table = (
        (numbers[:, None] == jnp.arange(expert_count, dtype=jnp.int32)[None, :]) & active[:, None]
    ).astype(jnp.int32)
    within = jnp.sum((jnp.cumsum(table, axis=0) - table) * table, axis=1)
    return (within, table)


def pack_rows(tokens, destination, active, slot_total, top_count):
    pick_number = jnp.arange(destination.shape[0], dtype=jnp.int32)
    match_grid = (
        destination[None, :] == jnp.arange(slot_total, dtype=jnp.int32)[:, None]
    ) & active[None, :]
    source = jnp.sum(jnp.where(match_grid, pick_number[None, :] + 1, 0), axis=1) - 1
    picked_rows = jnp.take(tokens, jnp.maximum(source, 0) // top_count, axis=0)
    return jnp.where((source >= 0)[:, None], picked_rows, jnp.zeros((), tokens.dtype))


def send_rows(slot_rows):
    return lax.all_to_all(slot_rows, ("gx", "gy"), split_axis=0, concat_axis=0, tiled=True)


def on_device(tokens, expert_ids, backup_ids, scores, gate_weight, up_weight, down_weight):
    device_count = lax.axis_size(("gx", "gy"))
    own_index = lax.axis_index(("gx", "gy"))
    tok_rows, top_count = expert_ids.shape
    model_width = tokens.shape[1]
    per_source = tok_rows * top_count
    spare_quota = max(1, per_source // (4 * device_count))
    most_rows = max(2, (3 * per_source + 2 * device_count - 1) // (2 * device_count))
    first_flat = expert_ids.reshape(-1)
    backup_flat = backup_ids.reshape(-1)
    everyone = jnp.ones((per_source,), dtype=bool)
    first_within, first_table = ranks_within(first_flat, everyone, device_count)
    own_counts = jnp.sum(first_table, axis=0)
    all_counts = lax.all_gather(own_counts[None, :], ("gx", "gy"), axis=0, tiled=True)
    before = jnp.cumsum(all_counts, axis=0) - all_counts
    own_before = lax.dynamic_index_in_dim(before, own_index, 0, keepdims=False)
    first_rank = jnp.sum(first_table * own_before[None, :], axis=1) + first_within
    kept_mask = first_rank < per_source
    spilled = jnp.logical_not(kept_mask)
    spill_rank = ranks_within(backup_flat, spilled, device_count)[0]
    spare_mask = spilled & (spill_rank < spare_quota)
    send_first = pack_rows(
        tokens,
        first_flat * most_rows + first_within,
        kept_mask,
        device_count * most_rows,
        top_count,
    ).reshape(device_count, most_rows, model_width)
    send_spill = pack_rows(
        tokens,
        backup_flat * spare_quota + spill_rank,
        spare_mask,
        device_count * spare_quota,
        top_count,
    ).reshape(device_count, spare_quota, model_width)
    recv_first = send_rows(send_first)
    recv_spill = send_rows(send_spill)
    count_column = lax.dynamic_index_in_dim(all_counts, own_index, 1, keepdims=False)
    before_column = lax.dynamic_index_in_dim(before, own_index, 1, keepdims=False)
    ending = before_column + count_column
    row_number = jnp.arange(per_source, dtype=jnp.int32)
    source_of_row = jnp.sum((ending[None, :] <= row_number[:, None]).astype(jnp.int32), axis=1)
    owner_grid = source_of_row[:, None] == jnp.arange(device_count, dtype=jnp.int32)[None, :]
    start_of_row = jnp.sum(jnp.where(owner_grid, before_column[None, :], 0), axis=1)
    filled = row_number < ending[device_count - 1]
    slot_index = jnp.minimum(source_of_row, device_count - 1) * most_rows + jnp.clip(
        row_number - start_of_row, 0, most_rows - 1
    )
    first_rows = jnp.take(
        recv_first.reshape(device_count * most_rows, model_width), slot_index, axis=0
    )
    first_rows = jnp.where(filled[:, None], first_rows, jnp.zeros((), first_rows.dtype))
    expert_rows = jnp.concatenate(
        [first_rows, recv_spill.reshape(device_count * spare_quota, model_width)], axis=0
    )
    gate = jnp.dot(expert_rows, gate_weight[0], preferred_element_type=jnp.float32)
    upward = jnp.dot(expert_rows, up_weight[0], preferred_element_type=jnp.float32)
    hidden = (jax.nn.silu(gate) * upward).astype(jnp.bfloat16)
    expert_out = jnp.dot(hidden, down_weight[0], preferred_element_type=jnp.float32).astype(
        jnp.bfloat16
    )
    position = jnp.arange(most_rows, dtype=jnp.int32)
    rank_grid = before_column[:, None] + position[None, :]
    live_slot = (position[None, :] < count_column[:, None]) & (rank_grid < per_source)
    back_first = jnp.take(expert_out[:per_source], jnp.clip(rank_grid, 0, per_source - 1), axis=0)
    back_first = jnp.where(live_slot[:, :, None], back_first, jnp.zeros((), back_first.dtype))
    back_spill = expert_out[per_source:].reshape(device_count, spare_quota, model_width)
    home_first = send_rows(back_first)
    home_spill = send_rows(back_spill)
    first_slot = jnp.minimum(first_flat * most_rows + first_within, device_count * most_rows - 1)
    spill_slot = backup_flat * spare_quota + jnp.minimum(spill_rank, spare_quota - 1)
    picked_first = jnp.take(
        home_first.reshape(device_count * most_rows, model_width), first_slot, axis=0
    )
    picked_spill = jnp.take(
        home_spill.reshape(device_count * spare_quota, model_width), spill_slot, axis=0
    )
    picked = jnp.where(kept_mask[:, None], picked_first, picked_spill).reshape(
        tok_rows, top_count, model_width
    )
    route_weights = scores / jnp.sum(scores, axis=1, keepdims=True)
    weights = jnp.where(
        (kept_mask | spare_mask).reshape(tok_rows, top_count),
        route_weights,
        jnp.zeros((), jnp.float32),
    )
    mixed = jnp.sum(weights[:, :, None] * picked.astype(jnp.float32), axis=1)
    return mixed.astype(jnp.bfloat16)


def exchange(cfg, tok_ref, ids_ref, backups_ref, scores_ref, gate_hbm, up_hbm, down_hbm, out_ref,
             flipped, metas, toks, wg, wu, wd, pick, comb_hi, comb_lo, gate, upward, hidden,
             own, to_core, from_core, to_one, from_one, to_two, from_two, to_z, from_z,
             meta_send, meta_recv, ag_send, ag_recv, rs_send, rs_recv, w_sem):
    parts, width, cap, quota, slots, top = cfg
    z = lax.axis_index("gx")
    g = lax.axis_index("gy")
    c = lax.rem(g, 2)
    x = lax.rem(lax.div(g, 2), 2)
    y = lax.div(g, 4)
    core_peer = (z, g + 1 - 2 * c)
    x_peer = (z, g + 2 - 4 * x)
    y_peer = (z, g + 4 - 8 * y)
    z_near = [z + 1 - 2 * lax.rem(z, 2), z + 2 - 4 * lax.div(z, 2), 3 - z]
    z_peers = [(there, g) for there in z_near]
    expert = z * 8 + g

    def remote(src, dst, sems, device):
        return pltpu.make_async_remote_copy(
            src_ref=src, dst_ref=dst, send_sem=sems[0], recv_sem=sems[1],
            device_id=device, device_id_type=pl.DeviceIdType.MESH)

    weight_copies = []
    for j in range(parts):
        rows = pl.ds(j * width, width)
        pair = [pltpu.make_async_copy(gate_hbm.at[0, rows], wg.at[rows], w_sem.at[0, j]),
                pltpu.make_async_copy(up_hbm.at[0, rows], wu.at[rows], w_sem.at[1, j])]
        weight_copies.append(pair)
    down_copies = []
    for j in range(parts):
        copy = pltpu.make_async_copy(down_hbm.at[0, :, pl.ds(j * width, width)], wd.at[j], w_sem.at[2, j])
        down_copies.append(copy)

    barrier = pltpu.get_barrier_semaphore()
    for peer in [core_peer, x_peer, y_peer] + z_peers:
        pl.semaphore_signal(barrier, inc=1, device_id=peer, device_id_type=pl.DeviceIdType.MESH)
    scores = scores_ref[...]
    flipped[0:3 * top, 0:16] = jnp.concatenate(
        [ids_ref[...].astype(jnp.float32), backups_ref[...].astype(jnp.float32),
         scores / jnp.sum(scores, axis=0, keepdims=True)], axis=0)
    metas[z, y, x, c] = flipped[...].T[0:16]
    for j in range(parts):
        toks[j, z, y, x, c] = tok_ref[:, j * width:(j + 1) * width]
    pl.semaphore_wait(barrier, 6)

    started = []

    def begin(group):
        for copy in group:
            copy.start()
            started.append(copy)

    def arrive(group):
        for copy in group:
            copy.wait_recv()

    def unit_copies(buf, send, recv, at, zz, flip):
        line, whole = buf.at[zz, y, x, c], buf.at[zz, :, :, c]
        plane = buf.at[zz, :, x, c] if flip else buf.at[zz, y, :, c]
        one, two = (y_peer, x_peer) if flip else (x_peer, y_peer)
        return [[remote(line, line, (send.at[at], recv.at[at]), one)],
                [remote(plane, plane, (send.at[at + 1], recv.at[at + 1]), two)],
                [remote(whole, whole, (send.at[at + 2], recv.at[at + 2]), core_peer)]]

    mine = metas.at[z, y, x, c]
    meta_z = [remote(mine, mine, (meta_send.at[k], meta_recv.at[k]), z_peers[k]) for k in range(3)]
    line, plane, whole = metas.at[:, y, x, c], metas.at[:, y, :, c], metas.at[:, :, :, c]
    meta_rest = [remote(part, part, (meta_send.at[3 + k], meta_recv.at[3 + k]), peer)
                 for k, (part, peer) in enumerate(((line, x_peer), (plane, y_peer), (whole, core_peer)))]
    token_z = []
    for j in range(parts):
        mine = toks.at[j, z, y, x, c]
        token_z.append([remote(mine, mine, (ag_send.at[j, k], ag_recv.at[j, k]), z_peers[k]) for k in range(3)])
    z_order = [z] + z_near
    units = [(p, b) for p in range(parts // 2) for b in range(4)]
    gathers = []
    for p, b in units:
        pair = [unit_copies(toks.at[j], ag_send.at[j], ag_recv.at[j], 3 + 3 * b, z_order[b], j % 2 == 1)
                for j in (2 * p, 2 * p + 1)]
        gathers.append([pair[0][stage] + pair[1][stage] for stage in range(3)])

    def route():
        record = metas[...].reshape(512, 128)
        first, backup, weight = record[:, 0:top], record[:, top:2 * top], record[:, 2 * top:3 * top]
        lane = lax.broadcasted_iota(jnp.int32, (512, 128), 1).astype(jnp.float32)
        named = jnp.zeros((512, 128), jnp.float32)
        for k in range(top):
            named += jnp.where(first[:, k:k + 1] == lane, 1.0, 0.0)
        row = lax.broadcasted_iota(jnp.int32, (512, 512), 0)
        col = lax.broadcasted_iota(jnp.int32, (512, 512), 1)
        lower = jnp.where(col < row, 1.0, 0.0)
        rank = jnp.dot(lower.astype(jnp.bfloat16), named.astype(jnp.bfloat16), preferred_element_type=jnp.float32)
        spilled = jnp.where(rank >= cap, named, 0.0)
        me = expert.astype(jnp.float32)
        is_me = jnp.where(lane == me, 1.0, 0.0)
        my_named = jnp.sum(is_me * named, axis=1, keepdims=True)
        my_rank = jnp.sum(is_me * rank, axis=1, keepdims=True)
        my_weight = jnp.sum(jnp.where(first == me, weight, 0.0), axis=1, keepdims=True)
        has_backup = jnp.sum(jnp.where(backup == me, 1.0, 0.0), axis=1, keepdims=True)
        its_first = jnp.sum(jnp.where(backup == me, first, 0.0), axis=1, keepdims=True)
        its_weight = jnp.sum(jnp.where(backup == me, weight, 0.0), axis=1, keepdims=True)
        moved = has_backup * jnp.sum(jnp.where(lane == its_first, spilled, 0.0), axis=1, keepdims=True)
        near = jnp.where(lax.div(row, 16) == lax.div(col, 16), lower, 0.0)
        moved_wide = jnp.broadcast_to(moved, (512, 128))
        spill_rank = jnp.dot(near.astype(jnp.bfloat16), moved_wide.astype(jnp.bfloat16),
                             preferred_element_type=jnp.float32)
        block = lax.div(lax.broadcasted_iota(jnp.int32, (512, 128), 0), 16).astype(jnp.float32)
        kept_grid = jnp.where(my_rank == lane, my_named, 0.0)
        spare_grid = jnp.where(spill_rank < quota, jnp.where(block * quota + spill_rank == lane, moved_wide, 0.0), 0.0)
        grid = jnp.concatenate([kept_grid, spare_grid], axis=1)
        pick[...] = grid.T[:slots].astype(jnp.bfloat16)
        mixing = jnp.concatenate([kept_grid * my_weight, spare_grid * its_weight], axis=1)[:, :slots]
        high = mixing.astype(jnp.bfloat16)
        comb_hi[...] = high.reshape(16, 2, 16, slots)
        comb_lo[...] = (mixing - high.astype(jnp.float32)).astype(jnp.bfloat16).reshape(16, 2, 16, slots)

    def project(j):
        for copy in weight_copies[j]:
            copy.wait()
        rows = jnp.dot(pick[...], toks[j].reshape(512, width), preferred_element_type=jnp.float32).astype(jnp.bfloat16)
        part = pl.ds(j * width, width)
        new_gate = jnp.dot(rows, wg[part, :], preferred_element_type=jnp.float32)
        new_up = jnp.dot(rows, wu[part, :], preferred_element_type=jnp.float32)
        if j == 0:
            gate[...] = new_gate
            upward[...] = new_up
        elif j < parts - 1:
            gate[...] += new_gate
            upward[...] += new_up
        else:
            full = gate[...] + new_gate
            hidden[...] = (full / (1.0 + jnp.exp(-full)) * (upward[...] + new_up)).astype(jnp.bfloat16)

    begin(meta_z)
    begin(gathers[0][0])
    for p in range(parts // 2):
        for k in range(3):
            begin([token_z[2 * p][k], token_z[2 * p + 1][k]])
    for copy in [copy for pair in weight_copies for copy in pair] + down_copies:
        copy.start()
    count = len(units)
    for step in range(count + 3):
        if step == 1:
            arrive(meta_z)
            begin(meta_rest[0:1])
        if 2 <= step <= 3:
            arrive(meta_rest[step - 2:step - 1])
            begin(meta_rest[step - 1:step])
        if 0 < step <= count:
            arrive(gathers[step - 1][0])
            begin(gathers[step - 1][1])
        if 0 < step < count:
            p, b = units[step]
            if b > 0:
                arrive([token_z[2 * p][b - 1], token_z[2 * p + 1][b - 1]])
            begin(gathers[step][0])
        if 0 <= step - 2 < count:
            arrive(gathers[step - 2][1])
            begin(gathers[step - 2][2])
        if step == 4:
            arrive(meta_rest[2:3])
            route()
        i = step - 3
        if 0 <= i < count:
            arrive(gathers[i][2])
            if units[i][1] == 3:
                project(2 * units[i][0])
                project(2 * units[i][0] + 1)

    core_copies = [remote(to_core.at[j], from_core.at[j], (rs_send.at[j, 0], rs_recv.at[j, 0]), core_peer)
                   for j in range(parts)]
    back_order = [z_near[2], z_near[1], z_near[0], z]

    def scatter_copies(j, b):
        zz = back_order[b]
        one, two = (y_peer, x_peer) if j % 2 == 0 else (x_peer, y_peer)
        sem = lambda k: (rs_send.at[j, k], rs_recv.at[j, k])
        copies = [remote(to_one.at[j, zz], from_one.at[j, zz], sem(1 + 3 * b), one),
                  remote(to_two.at[j, zz], from_two.at[j, zz], sem(2 + 3 * b), two)]
        if b < 3:
            copies.append(remote(to_z.at[j, b], from_z.at[j, b], sem(3 + 3 * b), z_peers[2 - b]))
        return copies

    scatters = [[scatter_copies(j, b) for j in (2 * p, 2 * p + 1)] for p, b in units]
    f32 = jnp.float32

    def produce(j):
        down_copies[j].wait()
        rows = jnp.dot(hidden[...], wd[j], preferred_element_type=f32).astype(jnp.bfloat16)

        def combine(core):
            high = comb_hi[:, core].reshape(256, slots)
            low = comb_lo[:, core].reshape(256, slots)
            return (jnp.dot(high, rows, preferred_element_type=f32) + jnp.dot(low, rows, preferred_element_type=f32))

        to_core[j] = combine(1 - c).astype(jnp.bfloat16).reshape(4, 2, 2, 16, width)
        begin([core_copies[j]])
        own[j] = combine(c).reshape(4, 2, 2, 16, width)

    def at_one(j, zz, first, second):
        yy, xx = (first, second) if j % 2 == 0 else (second, first)
        return own[j, zz, yy, xx] + from_core[j, zz, yy, xx].astype(f32)

    def after_core(j, zz):
        first = y if j % 2 == 0 else x
        for second in range(2):
            to_one[j, zz, second] = at_one(j, zz, 1 - first, second).astype(jnp.bfloat16)

    def at_two(j, zz, first, second):
        return at_one(j, zz, first, second) + from_one[j, zz, second].astype(f32)

    def after_one(j, zz):
        first, second = (y, x) if j % 2 == 0 else (x, y)
        to_two[j, zz] = at_two(j, zz, first, 1 - second).astype(jnp.bfloat16)

    def at_z(j, zz):
        first, second = (y, x) if j % 2 == 0 else (x, y)
        return at_two(j, zz, first, second) + from_two[j, zz].astype(f32)

    def finish(j):
        total = at_z(j, z)
        for k in range(3):
            total += from_z[j, k].astype(f32)
        out_ref[:, j * width:(j + 1) * width] = total.astype(jnp.bfloat16)

    produce(0)
    produce(1)
    for step in range(count + 3):
        if step < count:
            p, b = units[step]
            if b == 0:
                arrive(core_copies[2 * p:2 * p + 2])
            for h in range(2):
                after_core(2 * p + h, back_order[b])
                begin(scatters[step][h][0:1])
            if b == 1 and 2 * p + 2 < parts:
                produce(2 * p + 2)
                produce(2 * p + 3)
        i = step - 1
        if 0 <= i < count:
            p, b = units[i]
            for h in range(2):
                arrive(scatters[i][h][0:1])
                after_one(2 * p + h, back_order[b])
                begin(scatters[i][h][1:2])
        i = step - 2
        if 0 <= i < count:
            p, b = units[i]
            for h in range(2):
                arrive(scatters[i][h][1:2])
                if b < 3:
                    to_z[2 * p + h, b] = at_z(2 * p + h, back_order[b]).astype(jnp.bfloat16)
                    begin(scatters[i][h][2:3])
        i = step - 3
        if 0 <= i < count and units[i][1] == 3:
            for h in range(2):
                arrive([scatters[i - 3 + k][h][2] for k in range(3)])
                finish(2 * units[i][0] + h)

    for copy in started:
        copy.wait_send()


def fused_body(parts, tokens, expert_ids, backup_ids, scores, gate_weight, up_weight, down_weight):
    device_count = lax.axis_size(("gx", "gy"))
    tok_rows, top = expert_ids.shape
    model, ff = gate_weight.shape[1:]
    cap = tok_rows * top
    quota = max(1, cap // (4 * device_count))
    slots = cap + device_count * quota
    width = model // parts
    bf16, f32 = jnp.bfloat16, jnp.float32
    grid = (4, 2, 2)
    vmem = lambda shape, kind: pltpu.VMEM(shape, kind)
    scratch = [
        vmem((128, 128), f32), vmem(grid + (2, tok_rows, 128), f32),
        vmem((parts,) + grid + (2, tok_rows, width), bf16),
        vmem((model, ff), bf16), vmem((model, ff), bf16), vmem((parts, ff, width), bf16),
        vmem((slots, 512), bf16),
        vmem((16, 2, tok_rows, slots), bf16), vmem((16, 2, tok_rows, slots), bf16),
        vmem((slots, ff), f32), vmem((slots, ff), f32), vmem((slots, ff), bf16),
        vmem((parts,) + grid + (tok_rows, width), f32),
        vmem((parts,) + grid + (tok_rows, width), bf16), vmem((parts,) + grid + (tok_rows, width), bf16),
        vmem((parts, 4, 2, tok_rows, width), bf16), vmem((parts, 4, 2, tok_rows, width), bf16),
        vmem((parts, 4, tok_rows, width), bf16), vmem((parts, 4, tok_rows, width), bf16),
        vmem((parts, 3, tok_rows, width), bf16), vmem((parts, 3, tok_rows, width), bf16),
        pltpu.SemaphoreType.DMA((6,)), pltpu.SemaphoreType.DMA((6,)),
        pltpu.SemaphoreType.DMA((parts, 15)), pltpu.SemaphoreType.DMA((parts, 15)),
        pltpu.SemaphoreType.DMA((parts, 13)), pltpu.SemaphoreType.DMA((parts, 13)),
        pltpu.SemaphoreType.DMA((3, parts)),
    ]
    whole = pl.BlockSpec(memory_space=pltpu.VMEM)
    away = pl.BlockSpec(memory_space=pl.ANY)
    return pl.pallas_call(
        functools.partial(exchange, (parts, width, cap, quota, slots, top)),
        out_shape=jax.ShapeDtypeStruct((tok_rows, model), bf16),
        in_specs=[whole, whole, whole, whole, away, away, away],
        out_specs=whole,
        scratch_shapes=scratch,
        compiler_params=pltpu.CompilerParams(
            collective_id=0, has_side_effects=True, vmem_limit_bytes=60 * 1024 * 1024),
    )(tokens, expert_ids.T, backup_ids.T, scores.T, gate_weight, up_weight, down_weight)


def pick_body(mesh):
    if mesh.shape["gx"] == 4 and mesh.shape["gy"] == 8:
        return functools.partial(fused_body, 2)
    return on_device


def solution(mesh):
    placed = (
        P(("gx", "gy"), None),
        P(("gx", "gy"), None),
        P(("gx", "gy"), None),
        P(("gx", "gy"), None),
        P(("gx", "gy"), None, None),
        P(("gx", "gy"), None, None),
        P(("gx", "gy"), None, None),
    )
    return jax.shard_map(
        pick_body(mesh), mesh=mesh, in_specs=placed, out_specs=P(("gx", "gy"), None), check_vma=False
    )
```
